32 devices in a mesh: enc: 4 (over y, x), slab: 8 (over z, core).
Axes of the slice: x: 2, y: 2, z: 4, core: 2. Of those that a mesh axis runs over, the one named last changes fastest.
Arguments:
- tokens: bfloat16 [8192, 1024], P(('slab', 'enc')), may hold values from -6 to 6
- cotangent: bfloat16 [8192, 1024], P(('slab', 'enc')), may hold values from -6 to 6
- w_qkv: bfloat16 [1024, 3072], P('slab', 'enc'), may hold values from -0.5 to 0.5
- w_out: bfloat16 [1024, 1024], P('enc', 'slab'), may hold values from -0.1875 to 0.1875
- mod_scale: float32 [1024], replicated, may hold values from -0.5 to 0.5
- mod_shift: float32 [1024], replicated, may hold values from -0.5 to 0.5
- mod_gate: float32 [1024], replicated, may hold values from 0.5 to 1.5
- counts: int32 [16], P('slab'), may hold values from 64 to 512
- edge_index: int32 [16, 128], P('slab'), may hold values from 0 to 1023
Outputs:
- grad_tokens: bfloat16 [8192, 1024], P(('slab', 'enc'))
- grad_qkv: float32 [1024, 3072], P('slab', 'enc')
- grad_out: float32 [1024, 1024], P('enc', 'slab')
The draws below stay inside these ranges and needn't reach their ends.
Inputs may be any that keep to these rules, and one draw needn't show every extreme that they name: The first counts[w] slots of window w hold voxels; the rest are padding. `edge_index`: A row index within the preceding slab's 2 * 512 rows.
All inputs are finite; a program needn't handle non-finite values.
Results may differ from the reference program's by a relative error of at most 0.023.
Values may be sent and summed in bfloat16 or wider, within the bound.
No kernel may reach another device: no remote copies, remote signals or barrier semaphores. Data moves between devices by JAX's collectives and lax.ppermute only.
A program may use at most 64 MiB of HBM per device.

```python
import math
import jax
import jax.numpy as jnp
from jax import lax

D = 1024
HEADS = 16
HD = 64
WIN = 512
EDGE = 128
W_DEV = 2
NWIN = 16
TOKENS = 8192
N_ENC = 4


def common_direction(key):
    raw = jax.random.normal(jax.random.fold_in(key, 101), (D,), jnp.float32)
    raw = raw - jnp.mean(raw)
    return raw / jnp.sqrt(jnp.sum(raw * raw))


def draw_tokens(key, part):
    direction = common_direction(key)
    noise = jax.random.normal(jax.random.fold_in(key, 13), (TOKENS, D), jnp.float32)
    lowest = 0.55
    highest = 0.9
    noise = noise - jnp.sum(noise * direction[None, :], 1, keepdims=True) * direction[None, :]
    strength = jax.random.uniform(jax.random.fold_in(key, 14), (NWIN, 1), jnp.float32, lowest, highest)
    span = WIN // 8
    first = jax.random.randint(jax.random.fold_in(key, 15), (NWIN, 1), 0, span)
    second = (first + 1 + jax.random.randint(jax.random.fold_in(key, 16), (NWIN, 1), 0, span - 1)) % span
    position = jnp.arange(WIN, dtype=jnp.int32)[None, :]
    aligned = jnp.where(position == first, strength, jnp.where(position == second, strength - 0.005, 0.0))
    aligned = aligned.reshape(TOKENS, 1)
    rows = aligned * math.sqrt(D) * direction[None, :] + jnp.sqrt(1.0 - aligned * aligned) * noise
    return jnp.clip(rows, -6.0, 6.0).astype(jnp.bfloat16)


def draw_w_qkv(key, part):
    direction = common_direction(key)
    base = jax.random.normal(jax.random.fold_in(key, 22), (D, HEADS, 3, HD), jnp.float32)
    base = base / math.sqrt(D)
    head_dir = jax.random.normal(jax.random.fold_in(key, 23), (HEADS, HD), jnp.float32)
    head_dir = head_dir / jnp.sqrt(jnp.sum(head_dir * head_dir, 1, keepdims=True))
    strength = 1.8
    boost = strength * direction[:, None, None] * head_dir[None, :, :]
    extra = jnp.stack([boost, boost, jnp.zeros_like(boost)], 2)
    return jnp.clip(base + extra, -0.5, 0.5).reshape(D, 3 * D).astype(jnp.bfloat16)


def touch_ends(result, rng, low, high):
    longest = result.shape.index(max(result.shape))
    spots = []
    for shift in (0, 1):
        where = [jax.random.randint(jax.random.fold_in(rng, axis), (), 0, length) for axis, length in enumerate(result.shape)]
        where[longest] = (where[longest] + shift) % result.shape[longest]
        spots.append(tuple(where))
    return result.at[spots[0]].set(low).at[spots[1]].set(high)


def block_levels(own_key, shape, shards, least, high):
    loudness = 1.0
    for dim, shards_of in shards:
        heights = jax.random.uniform(jax.random.fold_in(jax.random.fold_in(own_key, 6), dim), (shards_of,), jnp.float32, least / len(shards), high / len(shards))
        loudness = loudness * jnp.repeat(jnp.exp(heights), shape[dim] // shards_of).reshape((-1,) + (1,) * (len(shape) - 1 - dim))
    return loudness


def scatter_about(rng, extent, scale, most, split=(), kind=jnp.bfloat16):
    result = scale * jax.random.normal(rng, extent, jnp.float32)
    if split:
        result = result * block_levels(rng, extent, split, -0.22, 0.18)
    return jnp.clip(result, -most, most).astype(kind)


def setup_inputs(seed: int = 0) -> dict:
    key_of = jax.random.split(jax.random.key(seed), 10)
    tokens = draw_tokens(jax.random.fold_in(key_of[9], 71), 0)
    cotangent = scatter_about(key_of[1], (TOKENS, D), 1.0, 6.0, ((0, 32),))
    w_qkv = draw_w_qkv(jax.random.fold_in(key_of[9], 71), 0)
    w_out = scatter_about(key_of[3], (D, D), D ** -0.5, 0.1875, ((0, 4), (1, 8)))
    mod_scale = jnp.clip(jax.random.uniform(key_of[4], (D,), jnp.float32, -0.5, 0.5), -0.5, 0.5)
    mod_shift = jnp.clip(jax.random.uniform(key_of[5], (D,), jnp.float32, -0.5, 0.5), -0.5, 0.5)
    mod_gate = jnp.clip(jax.random.uniform(key_of[6], (D,), jnp.float32, 0.5, 1.5), 0.5, 1.5)
    counts = touch_ends(jax.random.randint(key_of[7], (NWIN,), WIN // 8, WIN + 1), jax.random.fold_in(key_of[7], 1), WIN // 8, WIN).astype(jnp.int32)
    edge_index = touch_ends(jax.random.randint(key_of[8], (NWIN, EDGE), 0, W_DEV * WIN), jax.random.fold_in(key_of[8], 1), 0, (W_DEV * WIN) - 1).astype(jnp.int32)
    return {"tokens": tokens, "cotangent": cotangent, "w_qkv": w_qkv, "w_out": w_out, "mod_scale": mod_scale, "mod_shift": mod_shift, "mod_gate": mod_gate, "counts": counts, "edge_index": edge_index}


EPS = 1e-06

def rounded(value):
    return lax.optimization_barrier(value.astype(jnp.bfloat16)).astype(jnp.float32)

def statistics(features):
    widened = features.astype(jnp.float32)
    average = lax.optimization_barrier(jnp.mean(widened, 1, keepdims=True))
    centred = widened - average
    variance = lax.optimization_barrier(jnp.mean(centred * centred, 1, keepdims=True))
    inv_std = lax.rsqrt(variance + EPS)
    return (centred * inv_std, inv_std)

def attend(query, key_vals, edge_vals, counts, edge_live, upstream, out_rows):
    windows = counts.shape[0]
    row_count = query.shape[0]
    win_size = row_count // windows
    head_size = query.shape[1]
    factor = head_size ** (-0.5)
    query_win = query.reshape(windows, win_size, head_size).astype(jnp.float32)
    keys_all = jnp.concatenate([key_vals.reshape(windows, win_size, 2 * head_size), edge_vals], 1).astype(jnp.float32)
    key_part = keys_all[:, :, :head_size]
    value_part = keys_all[:, :, head_size:]
    position = jnp.arange(win_size, dtype=jnp.int32)
    own_live = position[None, :] < counts[:, None]
    key_live = jnp.concatenate([own_live, jnp.broadcast_to(edge_live[:, None], (windows, edge_vals.shape[1]))], 1)
    row_live = own_live.astype(jnp.float32)[:, :, None]
    scores = jnp.einsum('wqd,wkd->wqk', query_win, key_part) * factor
    scores = jnp.where(key_live[:, None, :], scores, -1000000000.0)
    largest = lax.optimization_barrier(jnp.max(scores, -1, keepdims=True))
    exponent = jnp.exp(scores - largest)
    softmax_p = exponent / lax.optimization_barrier(jnp.sum(exponent, -1, keepdims=True))
    weights_b = rounded(softmax_p)
    attended = (jnp.einsum('wqk,wkd->wqd', weights_b, value_part) * row_live).astype(jnp.bfloat16)
    attended = attended.reshape(row_count, head_size)
    grad_att = jnp.dot(upstream, out_rows.T, preferred_element_type=jnp.float32).reshape(windows, win_size, head_size)
    grad_att = rounded(grad_att * row_live)
    grad_prob = jnp.einsum('wqd,wkd->wqk', grad_att, value_part)
    grad_value = jnp.einsum('wqk,wqd->wkd', weights_b, grad_att)
    grad_score = rounded(softmax_p * (grad_prob - lax.optimization_barrier(jnp.sum(grad_prob * softmax_p, -1, keepdims=True))) * factor)
    grad_query = jnp.einsum('wqk,wkd->wqd', grad_score, key_part)
    grad_key = jnp.einsum('wqk,wqd->wkd', grad_score, query_win)
    grad_pair = jnp.concatenate([grad_key, grad_value], -1)
    own_pair = grad_pair[:, :win_size].reshape(row_count, 2 * head_size)
    return (attended, grad_query.reshape(row_count, head_size), own_pair, grad_pair[:, win_size:])

def reference(tokens, cotangent, w_qkv, w_out, mod_scale, mod_shift, mod_gate, counts, edge_index):
    row_block = W_DEV * WIN
    normal_x, inv_std = statistics(tokens)
    gain = 1.0 + mod_scale
    normed = (normal_x * gain + mod_shift).astype(jnp.bfloat16)
    upstream = (cotangent.astype(jnp.float32) * mod_gate).astype(jnp.bfloat16)
    windows = counts.shape[0]
    slab_of = jnp.arange(windows, dtype=jnp.int32) // W_DEV
    edge_rows = (jnp.maximum(slab_of - 1, 0) * row_block).astype(jnp.int32)[:, None] + edge_index
    flat_rows = edge_rows.reshape(-1).astype(jnp.int32)
    edge_live = slab_of > 0
    group_heads = HEADS // N_ENC
    wq_groups = w_qkv.reshape(D, N_ENC, group_heads * 3 * HD).transpose(1, 0, 2)
    wo_groups = w_out.reshape(N_ENC, group_heads * HD, D)

    def per_group(running, weights):
        weight_in, weight_out = weights
        projected = jnp.dot(normed, weight_in, preferred_element_type=jnp.float32).astype(jnp.bfloat16)
        pieces = []
        outputs = []
        for head_pos in range(group_heads):
            block = projected[:, head_pos * 3 * HD:(head_pos + 1) * 3 * HD]
            key_vals = block[:, HD:]
            edge_vals = key_vals[flat_rows].reshape(windows, EDGE, 2 * HD)
            attended, grad_query, own_pair, edge_pair = attend(block[:, :HD], key_vals, edge_vals, counts, edge_live, upstream, weight_out[head_pos * HD:(head_pos + 1) * HD])
            own_pair = own_pair.at[flat_rows].add(edge_pair.reshape(-1, 2 * HD))
            pieces.append(jnp.concatenate([grad_query, own_pair], 1))
            outputs.append(attended)
        grad_proj = jnp.concatenate(pieces, 1).astype(jnp.bfloat16)
        attended_all = jnp.concatenate(outputs, 1)
        grad_q = jnp.dot(normed.T, grad_proj, preferred_element_type=jnp.float32)
        grad_o = jnp.dot(attended_all.T, upstream, preferred_element_type=jnp.float32)
        partial_value = jnp.dot(grad_proj, weight_in.T, preferred_element_type=jnp.float32)
        return (running + rounded(partial_value), (grad_q, grad_o))
    start_sum = jnp.zeros((tokens.shape[0], D), jnp.float32)
    grad_normed, (grad_q_all, grad_o_all) = lax.scan(per_group, start_sum, (wq_groups, wo_groups))
    grad_hat = grad_normed * gain
    grad_tokens = cotangent.astype(jnp.float32) + inv_std * (grad_hat - lax.optimization_barrier(jnp.mean(grad_hat, 1, keepdims=True)) - normal_x * lax.optimization_barrier(jnp.mean(grad_hat * normal_x, 1, keepdims=True)))
    grad_qkv = grad_q_all.transpose(1, 0, 2).reshape(D, 3 * D)
    grad_out = grad_o_all.reshape(D, D)
    return (grad_tokens.astype(jnp.bfloat16), grad_qkv, grad_out)
```

```python
import functools
import jax
import jax.numpy as jnp
from jax import lax
from jax.experimental import pallas as pl
from jax.experimental.pallas import tpu as pltpu
from jax.sharding import PartitionSpec as P

HD = 64
EPS = 1e-06
F32 = jnp.float32
BF16 = jnp.bfloat16
NT = (((1,), (1,)), ((), ()))
TN = (((0,), (0,)), ((), ()))


def mm(a, b, dims=(((1,), (0,)), ((), ()))):
    return lax.dot_general(a, b, dims, preferred_element_type=F32)


def params(**kw):
    return pltpu.CompilerParams(**kw)


def swap(x, axis, mask):
    return lax.ppermute(x, axis, [(i, i ^ mask) for i in range(lax.axis_size(axis))])


def hop(x, axis, distance):
    n = lax.axis_size(axis)
    return lax.ppermute(x, axis, [(i, i + distance) for i in range(n) if 0 <= i + distance < n])


def turn(x, axis, distance):
    chips = lax.axis_size(axis) // 2
    return lax.ppermute(
        x,
        axis,
        [(2 * p + c, 2 * ((p + distance) % chips) + c) for p in range(chips) for c in range(2)],
    )


def gather_rows(x, axis):
    n = lax.axis_size(axis)
    if n == 4:
        half = x.shape[0] // 2
        one = swap(x, axis, 1)
        two = swap(x, axis, 2)
        three_a = swap(two[:half], axis, 1)
        three_b = swap(one[half:], axis, 2)
        return [x, one, two, three_a, three_b]
    pieces = [x]
    bit = 1
    while bit < n:
        pieces = pieces + [swap(piece, axis, bit) for piece in pieces]
        bit *= 2
    return pieces


def norm_kernel(tok_ref, cot_ref, scale_ref, shift_ref, gate_ref, normed_ref, up_ref):
    x = tok_ref[...].astype(F32)
    c = x - jnp.mean(x, 1, keepdims=True)
    var = jnp.mean(c * c, 1, keepdims=True)
    normal = c * lax.rsqrt(var + EPS)
    normed_ref[...] = (normal * (1.0 + scale_ref[...]) + shift_ref[...]).astype(BF16)
    up_ref[...] = (cot_ref[...].astype(F32) * gate_ref[...]).astype(BF16)


def relative_row(index, e, shift):
    return index ^ (e << shift)


def project_kernel(cfg, sc_ref, idx_ref, *refs):
    chips, pieces, heads, rows = cfg["chips"], cfg["pieces"], cfg["heads"], cfg["rows"]
    ws = refs[: 2 * chips]
    ns = refs[2 * chips : 2 * chips + pieces]
    q_ref, kv_ref, edge_ref, wq_ref, wo_ref = refs[2 * chips + pieces :]
    e, slab = sc_ref[0], sc_ref[1]
    p, c = slab // 2, slab % 2
    wr = ws[0].shape[0]
    qw = heads * 3 * HD
    half = heads * HD // 2
    for side in range(2):
        for t in range(chips):
            j = 2 * lax.rem(p - t + chips, chips) + (c ^ side)
            block = ws[side * chips + t]
            at = pl.multiple_of(j * wr, wr)
            wq_ref[pl.ds(at, wr), :] = block[:, :qw]
            wo_ref[j] = block[:, qw:]
    factor = HD ** (-0.5)
    off = 0
    for ref in ns:
        count = ref.shape[0]
        proj = mm(ref[...], wq_ref[...]).astype(BF16)
        for h in range(heads):
            q = proj[:, 3 * HD * h : 3 * HD * h + HD] * jnp.asarray(factor, BF16)
            q_ref[h, off : off + count, :] = jnp.concatenate([q, jnp.zeros_like(q)], 1)
            kv_ref[h, off : off + count, :] = proj[:, 3 * HD * h + HD : 3 * HD * (h + 1)]
        off += count
    want = relative_row(idx_ref[...], e, cfg["shift"])
    one_hot = (lax.broadcasted_iota(jnp.int32, (want.shape[0], rows), 1) == want).astype(F32).astype(BF16)
    for h in range(heads):
        edge_ref[:, 2 * HD * h : 2 * HD * (h + 1)] = mm(one_hot, kv_ref[h]).astype(BF16)


def attend_kernel(cfg, sc_ref, q_ref, kv_ref, edge_in_ref, wo_ref, *refs):
    pieces = cfg["pieces"]
    ups = refs[: len(pieces)]
    att_ref, dq_ref, dkv_ref, dedge_ref, ga_ref = refs[len(pieces) :]
    windows, win, shift, per = cfg["windows"], cfg["win"], cfg["shift"], cfg["per"]
    v, h = pl.program_id(0), pl.program_id(1)
    e, slab = sc_ref[0], sc_ref[1]
    w_abs = (e // per) ^ v
    count = sc_ref[2 + w_abs]
    low = (e % per) << shift
    live_q = (lax.broadcasted_iota(jnp.int32, (1, win), 1) ^ low) < count
    live_k = (lax.broadcasted_iota(jnp.int32, (win, 1), 0) ^ low) < count
    blocks, hd_half, wcol = wo_ref.shape[0], wo_ref.shape[1], wo_ref.shape[2] // 2

    for vv in range(windows):

        @pl.when((v == vv) & (h == 0))
        def _():
            off = 0
            for ref, count_rows in zip(ups, pieces):
                if off // win == vv:
                    at = off - vv * win
                    for part in range(2):
                        total = None
                        for j in range(blocks):
                            term = mm(
                                wo_ref[j, :, part * wcol : (part + 1) * wcol],
                                ref[:, j * wcol : (j + 1) * wcol],
                                NT,
                            )
                            total = term if total is None else total + term
                        ga_ref[part * hd_half : (part + 1) * hd_half, at : at + count_rows] = total
                off += count_rows

    q = q_ref[0]
    kv = jnp.concatenate([kv_ref[0], edge_in_ref[...]], 0)
    edges = edge_in_ref.shape[0]
    key_live = jnp.concatenate([live_k.astype(F32), jnp.full((edges, 1), jnp.where(slab > 0, 1.0, 0.0), F32)], 0)
    s = mm(kv, q, NT)
    s = jnp.where(key_live > 0.5, s, -1000000000.0)
    m = jnp.max(s, 0, keepdims=True)
    p = jnp.exp(s - m)
    inv = 1.0 / jnp.sum(p, 0, keepdims=True)
    pb = p.astype(BF16)
    kv_t = kv.T
    o_t = mm(kv_t, pb)[HD:] * inv
    live = live_q.astype(F32)
    att_ref[...] = (o_t * live).astype(BF16)
    g_t = (ga_ref[pl.ds(pl.multiple_of(h * HD, HD), HD), :] * live).astype(BF16)
    g_t = (g_t.astype(F32) * inv).astype(BF16)
    delta = jnp.sum(g_t.astype(F32) * o_t, 0, keepdims=True)
    g_pad = jnp.concatenate([jnp.zeros_like(g_t), g_t], 0)
    dp = mm(kv, g_pad)
    ds = (p * (dp - delta)).astype(BF16)
    dkv = mm(ds, q) + mm(pb, g_pad.T)
    dkv_ref[0] = dkv[:win]
    dedge_ref[...] = dkv[win:].astype(BF16)
    dq_t = mm(kv_t, ds)[:HD] * (HD ** (-0.5))
    dq_ref[0] = dq_t.T.astype(BF16)


def grads_kernel(cfg, sc_ref, idx_ref, edge_ref, dq_ref, dkv_ref, wq_ref, gp_ref, *outs):
    heads, rows, own = cfg["heads"], cfg["rows"], cfg["own"]
    want = relative_row(idx_ref[...], sc_ref[0], cfg["shift"])
    one_hot = (lax.broadcasted_iota(jnp.int32, (rows, want.shape[1]), 0) == want).astype(F32).astype(BF16)
    for h in range(heads):
        added = mm(one_hot, edge_ref[:, 2 * HD * h : 2 * HD * (h + 1)])
        pair = (dkv_ref[h] + added).astype(BF16)
        gp_ref[:, 3 * HD * h : 3 * HD * (h + 1)] = jnp.concatenate([dq_ref[h], pair], 1)
    for r in reversed(range(len(outs))):
        outs[r][...] = mm(gp_ref[r * own : (r + 1) * own, :], wq_ref[...], NT).astype(BF16)


def weights_kernel(cfg, sc_ref, gp_ref, att_ref, *refs):
    pieces = cfg["pieces"]
    ns, us = refs[: len(pieces)], refs[len(pieces) : 2 * len(pieces)]
    out_ref = refs[-1]
    qw = gp_ref.shape[1]
    half = att_ref.shape[0] // 2
    wr = out_ref.shape[2]
    total_q = None
    total_o = None
    off = 0
    for n_ref, u_ref, count in zip(ns, us, pieces):
        term = mm(n_ref[...], gp_ref[off : off + count, :], TN)
        total_q = term if total_q is None else total_q + term
        term = mm(att_ref[:, off : off + count], u_ref[...])
        total_o = term if total_o is None else total_o + term
        off += count
    out_ref[0, 0, :, :qw] = total_q.astype(BF16)
    out_ref[0, 0, :, qw : qw + wr] = total_o[:half].astype(BF16)
    out_ref[0, 0, :, qw + wr :] = total_o[half:].astype(BF16)


def final_kernel(tok_ref, cot_ref, scale_ref, *refs):
    parts, out_ref = refs[:-1], refs[-1]
    x = tok_ref[...].astype(F32)
    c = x - jnp.mean(x, 1, keepdims=True)
    inv = lax.rsqrt(jnp.mean(c * c, 1, keepdims=True) + EPS)
    normal = c * inv
    total = parts[0][...].astype(F32)
    for part in parts[1:]:
        total = total + part[...].astype(F32)
    hat = total * (1.0 + scale_ref[...])
    grad = hat - jnp.mean(hat, 1, keepdims=True) - normal * jnp.mean(hat * normal, 1, keepdims=True)
    out_ref[...] = (cot_ref[...].astype(F32) + inv * grad).astype(BF16)


def sum_kernel(qw, *refs):
    parts, (q_ref, o_ref) = refs[:-2], refs[-2:]
    total = parts[0][...].astype(F32)
    for part in parts[1:]:
        total = total + part[...].astype(F32)
    q_ref[...] = total[:, :qw]
    half, wr = o_ref.shape[0] // 2, o_ref.shape[1]
    o_ref[:half] = total[:, qw : qw + wr]
    o_ref[half:] = total[:, qw + wr :]


def weight_parts(gp, att, normed, upstream, slab, chips, wr):
    all_normed, all_up = jnp.concatenate(normed, 0), jnp.concatenate(upstream, 0)
    total_q = mm(all_normed, gp, TN).reshape(chips, 2, wr, -1)
    total_o = mm(att, all_up)
    total_o = total_o.reshape(2, -1, chips, 2, wr).transpose(2, 3, 1, 0, 4).reshape(chips, 2, wr, -1)
    total = jnp.concatenate([total_q, total_o], -1).astype(BF16).swapaxes(0, 1)
    total = jnp.roll(total, -(slab // 2), 1)
    own_side = lax.dynamic_index_in_dim(total, slab % 2, 0, False)
    other_side = lax.dynamic_index_in_dim(total, 1 - slab % 2, 0, False)
    return jnp.stack([other_side, own_side])


def shape(dims, dtype):
    return jax.ShapeDtypeStruct(tuple(dims), dtype)


SMEM = pl.BlockSpec(memory_space=pltpu.SMEM)
VMEM = pl.BlockSpec(memory_space=pltpu.VMEM)


def on_device(tokens, cotangent, w_qkv, w_out, mod_scale, mod_shift, mod_gate, counts, edge_index):
    n_enc, n_slab = lax.axis_size("enc"), lax.axis_size("slab")
    chips = n_slab // 2
    own, width = tokens.shape
    rows = own * n_enc
    windows, edges = edge_index.shape
    win = rows // windows
    per = n_enc // windows
    shift = own.bit_length() - 1
    heads = w_out.shape[0] // HD
    qw = w_qkv.shape[1]
    wr = w_qkv.shape[0]
    half = w_out.shape[0] // 2
    pair = 2 * HD * heads

    scale, mod_shift, gate = (a.reshape(1, width) for a in (mod_scale, mod_shift, mod_gate))
    e, slab = lax.axis_index("enc"), lax.axis_index("slab")
    scalars = jnp.concatenate([jnp.stack([e, slab]).astype(jnp.int32), counts])

    normed_own, up_own = pl.pallas_call(
        norm_kernel, out_shape=(shape(tokens.shape, BF16),) * 2, name="norm"
    )(tokens, cotangent, scale, mod_shift, gate)
    normed = gather_rows(normed_own, "enc")

    packed = jnp.concatenate([w_qkv, w_out[:half], w_out[half:]], 1)
    ring = [packed] + [turn(packed, "slab", t) for t in range(1, chips)]
    weights = ring + [swap(block, "slab", 1) for block in ring]
    idx_next = hop(edge_index, "slab", -1)

    upstream = gather_rows(up_own, "enc")
    pieces = tuple(piece.shape[0] for piece in normed)

    cfg = dict(
        chips=chips, pieces=len(pieces), heads=heads, rows=rows, shift=shift
    )
    q, kv, edge_out, wq, wo = pl.pallas_call(
        functools.partial(project_kernel, cfg),
        out_shape=(
            shape((heads, rows, 2 * HD), BF16),
            shape((heads, rows, 2 * HD), BF16),
            shape((windows * edges, pair), BF16),
            shape((width, qw), BF16),
            shape((n_slab, wr, packed.shape[1] - qw), BF16),
        ),
        in_specs=[SMEM] + [VMEM] * (1 + 2 * chips + len(pieces)),
        name="project",
    )(scalars, idx_next.reshape(-1, 1), *weights, *normed)
    edge_in = hop(edge_out, "slab", 1)

    cfg = dict(pieces=pieces, windows=windows, win=win, shift=shift, per=per)
    att, dq, dkv, dedge = pl.pallas_call(
        functools.partial(attend_kernel, cfg),
        grid_spec=pltpu.PrefetchScalarGridSpec(
            num_scalar_prefetch=1,
            grid=(windows, heads),
            in_specs=[
                pl.BlockSpec((1, win, 2 * HD), lambda v, h, sc: (h, v, 0)),
                pl.BlockSpec((1, win, 2 * HD), lambda v, h, sc: (h, v, 0)),
                pl.BlockSpec((edges, 2 * HD), lambda v, h, sc: ((sc[0] // per) ^ v, h)),
                pl.BlockSpec(wo.shape, lambda v, h, sc: (0, 0, 0)),
            ]
            + [pl.BlockSpec((count, width), lambda v, h, sc: (0, 0)) for count in pieces],
            out_specs=[
                pl.BlockSpec((HD, win), lambda v, h, sc: (h, v)),
                pl.BlockSpec((1, win, HD), lambda v, h, sc: (h, v, 0)),
                pl.BlockSpec((1, win, 2 * HD), lambda v, h, sc: (h, v, 0)),
                pl.BlockSpec((edges, 2 * HD), lambda v, h, sc: ((sc[0] // per) ^ v, h)),
            ],
            scratch_shapes=[pltpu.VMEM((heads * HD, win), F32)],
        ),
        out_shape=(
            shape((heads * HD, rows), BF16),
            shape((heads, rows, HD), BF16),
            shape((heads, rows, 2 * HD), F32),
            shape((windows * edges, pair), BF16),
        ),
        name="attend",
    )(scalars, q, kv, edge_in, wo, *upstream)
    dedge_in = hop(dedge, "slab", -1)

    cfg = dict(heads=heads, rows=rows, own=own, shift=shift)
    gp, *partial = pl.pallas_call(
        functools.partial(grads_kernel, cfg),
        out_shape=(shape((rows, qw), BF16),) + (shape((own, width), BF16),) * n_enc,
        in_specs=[SMEM] + [VMEM] * 5,
        name="grads",
    )(scalars, idx_next.reshape(1, -1), dedge_in, dq, dkv, wq)
    mine = [partial[0]] + [swap(partial[r], "enc", r) for r in range(1, n_enc)]

    def column(side, t, sc):
        p, c = sc[1] // 2, sc[1] % 2
        return 2 * lax.rem(p + t, chips) + (c ^ (1 - side))

    if wr % 128:
        local = weight_parts(gp, att, normed, upstream, slab, chips, wr)
    else:
        local = pl.pallas_call(
            functools.partial(weights_kernel, dict(pieces=pieces)),
            grid_spec=pltpu.PrefetchScalarGridSpec(
                num_scalar_prefetch=1,
                grid=(2, chips),
                in_specs=[
                    pl.BlockSpec((rows, qw), lambda s, t, sc: (0, 0)),
                    pl.BlockSpec((heads * HD, rows), lambda s, t, sc: (0, 0)),
                ]
                + [pl.BlockSpec((count, wr), lambda s, t, sc: (0, column(s, t, sc))) for count in pieces] * 2,
                out_specs=pl.BlockSpec((1, 1, wr, packed.shape[1]), lambda s, t, sc: (s, t, 0, 0)),
            ),
            out_shape=shape((2, chips, wr, packed.shape[1]), BF16),
            name="weights",
        )(scalars, gp, att, *normed, *upstream)
    other = swap(local[0], "slab", 1)
    both = [(local[1, t].astype(F32) + other[t].astype(F32)).astype(BF16) for t in range(chips)]
    arrived = [both[0]] + [turn(both[t], "slab", t) for t in range(1, chips)]
    grad_qkv, grad_out = pl.pallas_call(
        functools.partial(sum_kernel, qw),
        out_shape=(shape(w_qkv.shape, F32), shape(w_out.shape, F32)),
        name="total",
    )(*arrived)

    grad_tokens = pl.pallas_call(
        final_kernel, out_shape=shape(tokens.shape, BF16), name="final"
    )(tokens, cotangent, scale, *mine)
    return (grad_tokens, grad_qkv, grad_out)


def solution(mesh):
    placed = (
        P(("slab", "enc"), None),
        P(("slab", "enc"), None),
        P("slab", "enc"),
        P("enc", "slab"),
        P(),
        P(),
        P(),
        P("slab"),
        P("slab", None),
    )
    return jax.shard_map(
        on_device,
        mesh=mesh,
        in_specs=placed,
        out_specs=(P(("slab", "enc"), None), P("slab", "enc"), P("enc", "slab")),
        check_vma=False,
    )
```

```python
import functools
import jax
import jax.numpy as jnp
from jax import lax
from jax.experimental import pallas as pl
from jax.experimental.pallas import tpu as pltpu
from jax.sharding import PartitionSpec as P


HD = 64
EPS = 1e-06
F32 = jnp.float32
BF16 = jnp.bfloat16
NT = (((1,), (1,)), ((), ()))
TN = (((0,), (0,)), ((), ()))


def mm(a, b, dims=(((1,), (0,)), ((), ()))):
    return lax.dot_general(a, b, dims, preferred_element_type=F32)


def swap(x, axis, mask):
    return lax.ppermute(x, axis, [(i, i ^ mask) for i in range(lax.axis_size(axis))])


def hop(x, axis, distance):
    n = lax.axis_size(axis)
    pairs = [(i, i + distance) for i in range(n) if 0 <= i + distance < n]
    return lax.ppermute(x, axis, pairs)


def turn(x, axis, distance):
    chips = lax.axis_size(axis) // 2
    pairs = [(2 * p + c, 2 * ((p + distance) % chips) + c) for p in range(chips) for c in range(2)]
    return lax.ppermute(x, axis, pairs)


def gather_rows(x, axis, relay):
    n = lax.axis_size(axis)
    if n == 4:
        half = x.shape[0] // 2
        one = swap(x, axis, 1)
        two = swap(x, axis, 2)
        if relay:
            three = [swap(two[:half], axis, 1), swap(one[half:], axis, 2)]
        else:
            three = [swap(x, axis, 3)]
        return [x, one, two] + three
    pieces = [x]
    bit = 1
    while bit < n:
        pieces = pieces + [swap(piece, axis, bit) for piece in pieces]
        bit *= 2
    return pieces


def norm_kernel(tok_ref, cot_ref, scale_ref, shift_ref, gate_ref, normed_ref, up_ref):
    x = tok_ref[...].astype(F32)
    c = x - jnp.mean(x, 1, keepdims=True)
    var = jnp.mean(c * c, 1, keepdims=True)
    normal = c * lax.rsqrt(var + EPS)
    normed_ref[...] = (normal * (1.0 + scale_ref[...]) + shift_ref[...]).astype(BF16)
    up_ref[...] = (cot_ref[...].astype(F32) * gate_ref[...]).astype(BF16)


def relative_row(index, e, shift):
    return index ^ (e << shift)


def project_kernel(cfg, sc_ref, idx_ref, *refs):
    chips, pieces, heads, rows = cfg["chips"], cfg["pieces"], cfg["heads"], cfg["rows"]
    ws = refs[: 2 * chips]
    ns = refs[2 * chips : 2 * chips + pieces]
    q_ref, kv_ref, edge_ref, wq_ref = refs[2 * chips + pieces :]
    e, slab = sc_ref[0], sc_ref[1]
    p, c = slab // 2, slab % 2
    wr = ws[0].shape[0]
    for side in range(2):
        for t in range(chips):
            j = 2 * lax.rem(p - t + chips, chips) + (c ^ side)
            block = ws[side * chips + t]
            at = pl.multiple_of(j * wr, wr)
            wq_ref[pl.ds(at, wr), :] = block[...]
    factor = HD ** (-0.5)
    off = 0
    for ref in ns:
        count = ref.shape[0]
        proj = mm(ref[...], wq_ref[...]).astype(BF16)
        for h in range(heads):
            q = proj[:, 3 * HD * h : 3 * HD * h + HD] * jnp.asarray(factor, BF16)
            q_ref[h, off : off + count, :] = jnp.concatenate([q, jnp.zeros_like(q)], 1)
            kv_ref[h, off : off + count, :] = proj[:, 3 * HD * h + HD : 3 * HD * (h + 1)]
        off += count
    want = relative_row(idx_ref[...], e, cfg["shift"])
    one_hot = (lax.broadcasted_iota(jnp.int32, (want.shape[0], rows), 1) == want).astype(F32).astype(BF16)
    for h in range(heads):
        edge_ref[h] = mm(one_hot, kv_ref[h]).astype(BF16)


def lives(cfg, sc_ref, v):
    per, shift, win = cfg["per"], cfg["shift"], cfg["win"]
    e = sc_ref[0]
    count = sc_ref[2 + ((e // per) ^ v)]
    low = (e % per) << shift
    live_q = (lax.broadcasted_iota(jnp.int32, (1, win), 1) ^ low) < count
    live_k = (lax.broadcasted_iota(jnp.int32, (win, 1), 0) ^ low) < count
    return live_q, live_k


def units(heads, windows, body):
    def step(h, carry):
        for v in range(windows):
            body(h, v)
        return carry

    lax.fori_loop(0, heads, step, 0)


def sized(h, count):
    return pl.ds(pl.multiple_of(h * count, count), count)


def own_forward_kernel(cfg, sc_ref, q_ref, kv_ref, p_ref, m_ref, l_ref, o_ref):
    win = cfg["win"]
    live = [lives(cfg, sc_ref, v)[1] for v in range(cfg["windows"])]

    def body(h, v):
        at = slice(v * win, (v + 1) * win)
        kv = kv_ref[h, at, :]
        s = jnp.where(live[v], mm(kv, q_ref[h, at, :], NT), -1000000000.0)
        m = jnp.max(s, 0, keepdims=True)
        p = jnp.exp(s - m)
        pb = p.astype(BF16)
        m_ref[h, v] = m
        l_ref[h, v] = jnp.sum(p, 0, keepdims=True)
        p_ref[h, v] = pb
        o_ref[h, v] = mm(kv.T, pb)[HD:]

    units(q_ref.shape[0], cfg["windows"], body)


def scaled(g, by):
    part = (g * by).astype(BF16)
    return jnp.concatenate([jnp.zeros_like(part), part], 0)


def edge_kernel(cfg, sc_ref, q_ref, edge_ref, m_ref, l_ref, o_ref, wo_ref, *refs):
    pieces, windows, win, edges = cfg["pieces"], cfg["windows"], cfg["win"], cfg["edges"]
    ups = refs[: len(pieces)]
    att_ref, dedge_ref, dq_ref, g_ref, delta_ref, ga_ref, wos_ref = refs[len(pieces) :]
    chips, wcol = wo_ref.shape[0], wo_ref.shape[3]
    chip, core = sc_ref[1] // 2, sc_ref[1] % 2
    for t in range(chips):
        for side in range(2):
            j = 2 * lax.rem(chip - t + chips, chips) + (core ^ side)
            wos_ref[j] = wo_ref[t, side]
    off = 0
    for ref, count_rows in zip(ups, pieces):
        total = None
        for j in range(2 * chips):
            term = mm(wos_ref[j], ref[:, j * wcol : (j + 1) * wcol], NT)
            total = term if total is None else total + term
        ga_ref[:, off : off + count_rows] = total
        off += count_rows

    live = [lives(cfg, sc_ref, v)[0].astype(F32) for v in range(windows)]
    place = [(sc_ref[0] // cfg["per"]) ^ v for v in range(windows)]
    has_edges = sc_ref[1] > 0

    def body(h, v):
        at = slice(v * win, (v + 1) * win)
        kv = edge_ref[h, sized(place[v], edges), :]
        q = q_ref[h, at, :]
        s = jnp.where(has_edges, mm(kv, q, NT), -1000000000.0)
        m_edge = jnp.max(s, 0, keepdims=True)
        p = jnp.exp(s - m_edge)
        m_own = m_ref[h, v]
        m = jnp.maximum(m_own, m_edge)
        a, b = jnp.exp(m_own - m), jnp.exp(m_edge - m)
        inv = 1.0 / (a * l_ref[h, v] + b * jnp.sum(p, 0, keepdims=True))
        a, b = a * inv, b * inv
        kv_t = kv.T
        pb = p.astype(BF16)
        o = a * o_ref[h, v] + b * mm(kv_t, pb)[HD:]
        att_ref[sized(h, HD), at] = (o * live[v]).astype(BF16)
        gb = (ga_ref[sized(h, HD), at] * live[v]).astype(BF16)
        g = gb.astype(F32)
        delta = jnp.sum(g * o, 0, keepdims=True)
        g_pad = scaled(g, b)
        ds = (p * (mm(kv, g_pad) - b * delta)).astype(BF16)
        dedge_ref[h, sized(place[v], edges), :] = (mm(ds, q) + mm(pb, g_pad.T)).astype(BF16)
        dq_ref[h, v] = mm(kv_t, ds)[:HD]
        g_ref[h, v] = (g * a).astype(BF16)
        delta_ref[h, v] = a * delta

    units(q_ref.shape[0], windows, body)


def own_backward_kernel(cfg, sc_ref, q_ref, kv_ref, p_ref, g_ref, delta_ref, dqe_ref, dq_ref, dkv_ref):
    win = cfg["win"]

    def body(h, v):
        at = slice(v * win, (v + 1) * win)
        kv, pb, g = kv_ref[h, at, :], p_ref[h, v], g_ref[h, v]
        g_pad = jnp.concatenate([jnp.zeros_like(g), g], 0)
        ds = (pb.astype(F32) * (mm(kv, g_pad) - delta_ref[h, v])).astype(BF16)
        dkv_ref[h, at, :] = mm(ds, q_ref[h, at, :]) + mm(pb, g_pad.T)
        dq_t = (mm(kv.T, ds)[:HD] + dqe_ref[h, v]) * (HD ** (-0.5))
        dq_ref[h, at, :] = dq_t.T.astype(BF16)

    units(q_ref.shape[0], cfg["windows"], body)


def grads_kernel(cfg, sc_ref, idx_ref, edge_ref, dq_ref, dkv_ref, wq_ref, gp_ref, *outs):
    heads, rows, own = cfg["heads"], cfg["rows"], cfg["own"]
    want = relative_row(idx_ref[...], sc_ref[0], cfg["shift"])
    one_hot = (lax.broadcasted_iota(jnp.int32, (rows, want.shape[1]), 0) == want).astype(F32).astype(BF16)
    for h in range(heads):
        added = mm(one_hot, edge_ref[h])
        pair = (dkv_ref[h] + added).astype(BF16)
        gp_ref[:, 3 * HD * h : 3 * HD * (h + 1)] = jnp.concatenate([dq_ref[h], pair], 1)
    for r in reversed(range(len(outs))):
        outs[r][...] = mm(gp_ref[r * own : (r + 1) * own, :], wq_ref[...], NT).astype(BF16)


def place(sc_ref, j, chips):
    chip, core = sc_ref[1] // 2, sc_ref[1] % 2
    return ((j % 2) ^ core) ^ 1, lax.rem(j // 2 - chip + chips, chips)


def weights_in_kernel(pieces, sc_ref, gp_ref, *refs):
    ns, out_ref = refs[:-1], refs[-1]
    chips, wr = out_ref.shape[1], out_ref.shape[2]
    total = None
    off = 0
    for n_ref, count in zip(ns, pieces):
        term = mm(n_ref[...], gp_ref[off : off + count, :], TN)
        total = term if total is None else total + term
        off += count
    total = total.astype(BF16)
    for j in range(2 * chips):
        side, t = place(sc_ref, j, chips)
        out_ref[side, t] = total[j * wr : (j + 1) * wr]


def weights_out_kernel(pieces, sc_ref, att_ref, *refs):
    us, out_ref = refs[:-1], refs[-1]
    chips, wr = out_ref.shape[1], out_ref.shape[3]
    total = None
    off = 0
    for u_ref, count in zip(us, pieces):
        term = mm(att_ref[:, off : off + count], u_ref[...])
        total = term if total is None else total + term
        off += count
    total = total.astype(BF16)
    for j in range(2 * chips):
        side, t = place(sc_ref, j, chips)
        out_ref[side, t] = total[:, j * wr : (j + 1) * wr]


def add_kernel(mine_ref, other_ref, *outs):
    for t, out in enumerate(outs):
        out[...] = (mine_ref[1, t].astype(F32) + other_ref[t].astype(F32)).astype(BF16)


def final_kernel(tok_ref, cot_ref, scale_ref, *refs):
    parts, out_ref = refs[:-1], refs[-1]
    x = tok_ref[...].astype(F32)
    c = x - jnp.mean(x, 1, keepdims=True)
    inv = lax.rsqrt(jnp.mean(c * c, 1, keepdims=True) + EPS)
    normal = c * inv
    total = parts[0][...].astype(F32)
    for part in parts[1:]:
        total = total + part[...].astype(F32)
    hat = total * (1.0 + scale_ref[...])
    grad = hat - jnp.mean(hat, 1, keepdims=True) - normal * jnp.mean(hat * normal, 1, keepdims=True)
    out_ref[...] = (cot_ref[...].astype(F32) + inv * grad).astype(BF16)


def sum_kernel(chips, *refs):
    for first, out in ((0, refs[-2]), (chips, refs[-1])):
        total = refs[first][...].astype(F32)
        for part in refs[first + 1 : first + chips]:
            total = total + part[...].astype(F32)
        out[...] = total


def shape(dims, dtype):
    return jax.ShapeDtypeStruct(tuple(dims), dtype)


SMEM = pl.BlockSpec(memory_space=pltpu.SMEM)
VMEM = pl.BlockSpec(memory_space=pltpu.VMEM)


def call(kernel, outs, operands, scratch=(), limit=32):
    specs = [SMEM if operand.ndim == 1 else VMEM for operand in operands]
    return pl.pallas_call(
        kernel,
        out_shape=list(outs),
        in_specs=specs,
        out_specs=[VMEM] * len(outs),
        scratch_shapes=list(scratch),
        compiler_params=pltpu.CompilerParams(vmem_limit_bytes=limit * 2**20),
    )(*operands)


def scatter_slabs(parts, chips):
    other = swap(parts[0], "slab", 1)
    dims = parts.shape[2:]
    both = call(add_kernel, [shape(dims, BF16)] * chips, [parts, other])
    return [both[0]] + [turn(both[t], "slab", t) for t in range(1, chips)]


def program(tokens, cotangent, w_qkv, w_out, mod_scale, mod_shift, mod_gate, counts, edge_index):
    n_enc, n_slab = lax.axis_size("enc"), lax.axis_size("slab")
    chips = n_slab // 2
    own, width = tokens.shape
    rows = own * n_enc
    windows, edges = edge_index.shape
    win = rows // windows
    per = n_enc // windows
    shift = own.bit_length() - 1
    heads = w_out.shape[0] // HD
    qw = w_qkv.shape[1]
    wr = w_qkv.shape[0]

    scale, mod_shift, gate = (a.reshape(1, width) for a in (mod_scale, mod_shift, mod_gate))
    e, slab = lax.axis_index("enc"), lax.axis_index("slab")
    scalars = jnp.concatenate([jnp.stack([e, slab]).astype(jnp.int32), counts])

    ring = [w_qkv] + [turn(w_qkv, "slab", t) for t in range(1, chips)]
    normed_own, up_own = call(norm_kernel, [shape(tokens.shape, BF16)] * 2, [tokens, cotangent, scale, mod_shift, gate])
    normed = gather_rows(normed_own, "enc", True)
    idx_next = hop(edge_index, "slab", -1)
    weights = ring + [swap(block, "slab", 1) for block in ring]
    upstream = gather_rows(up_own, "enc", False)
    out_pair = jnp.stack([w_out, swap(w_out, "slab", 1)])
    out_ring = [out_pair] + [turn(out_pair, "slab", t) for t in range(1, chips)]
    n_pieces = tuple(piece.shape[0] for piece in normed)
    u_pieces = tuple(piece.shape[0] for piece in upstream)

    cfg = dict(chips=chips, pieces=len(normed), heads=heads, rows=rows, shift=shift)
    edge_shape = shape((heads, windows * edges, 2 * HD), BF16)
    q, kv, edge_out, wq = call(
        functools.partial(project_kernel, cfg),
        [shape((heads, rows, 2 * HD), BF16)] * 2 + [edge_shape, shape((width, qw), BF16)],
        [scalars, idx_next.reshape(-1, 1), *weights, *normed],
    )
    edge_in = hop(edge_out, "slab", 1)

    cfg = dict(windows=windows, win=win, shift=shift, per=per, edges=edges, pieces=u_pieces)
    line = shape((heads, windows, 1, win), F32)
    across = (heads, windows, HD, win)
    p, m, l, o = call(
        functools.partial(own_forward_kernel, cfg),
        [shape((heads, windows, win, win), BF16), line, line, shape(across, F32)],
        [scalars, q, kv],
    )
    wo = jnp.stack(out_ring)
    att, dedge, dqe, g, delta = call(
        functools.partial(edge_kernel, cfg),
        [shape((heads * HD, rows), BF16), edge_shape, shape(across, F32), shape(across, BF16), line],
        [scalars, q, edge_in, m, l, o, wo, *upstream],
        [pltpu.VMEM((heads * HD, rows), F32), pltpu.VMEM((n_slab,) + w_out.shape, BF16)],
    )
    dedge_in = hop(dedge, "slab", -1)
    (out_parts,) = call(
        functools.partial(weights_out_kernel, u_pieces),
        [shape((2, chips) + w_out.shape, BF16)],
        [scalars, att, *upstream],
    )
    out_arrived = scatter_slabs(out_parts, chips)
    dq, dkv = call(
        functools.partial(own_backward_kernel, cfg),
        [shape((heads, rows, HD), BF16), shape((heads, rows, 2 * HD), F32)],
        [scalars, q, kv, p, g, delta, dqe],
    )

    cfg = dict(heads=heads, rows=rows, own=own, shift=shift)
    gp, *partial = call(
        functools.partial(grads_kernel, cfg),
        [shape((rows, qw), BF16)] + [shape((own, width), BF16)] * n_enc,
        [scalars, idx_next.reshape(1, -1), dedge_in, dq, dkv, wq],
    )
    mine = [partial[0]] + [swap(partial[r], "enc", r) for r in range(1, n_enc)]
    (in_parts,) = call(
        functools.partial(weights_in_kernel, n_pieces), [shape((2, chips, wr, qw), BF16)], [scalars, gp, *normed]
    )
    in_arrived = scatter_slabs(in_parts, chips)
    grad_qkv, grad_out = call(
        functools.partial(sum_kernel, chips),
        [shape(w_qkv.shape, F32), shape(w_out.shape, F32)],
        [*in_arrived, *out_arrived],
    )
    (grad_tokens,) = call(final_kernel, [shape(tokens.shape, BF16)], [tokens, cotangent, scale, *mine])
    return (grad_tokens, grad_qkv, grad_out)


def solution(mesh):
    placed = (
        P(("slab", "enc"), None),
        P(("slab", "enc"), None),
        P("slab", "enc"),
        P("enc", "slab"),
        P(),
        P(),
        P(),
        P("slab"),
        P("slab", None),
    )
    return jax.shard_map(
        program,
        mesh=mesh,
        in_specs=placed,
        out_specs=(P(("slab", "enc"), None), P("slab", "enc"), P("enc", "slab")),
        check_vma=False,
    )
```

```python
import functools
import jax
import jax.numpy as jnp
from jax import lax
from jax.experimental import pallas as pl
from jax.experimental.pallas import tpu as pltpu
from jax.sharding import PartitionSpec as P


HD = 64
EPS = 1e-06
F32 = jnp.float32
BF16 = jnp.bfloat16
NT = (((1,), (1,)), ((), ()))
TN = (((0,), (0,)), ((), ()))


def mm(a, b, dims=(((1,), (0,)), ((), ()))):
    return lax.dot_general(a, b, dims, preferred_element_type=F32)


def joined(refs):
    return jnp.concatenate([ref[...] for ref in refs], 0)


def swap(x, axis, mask):
    return lax.ppermute(x, axis, [(i, i ^ mask) for i in range(lax.axis_size(axis))])


def hop(x, axis, distance):
    n = lax.axis_size(axis)
    pairs = [(i, i + distance) for i in range(n) if 0 <= i + distance < n]
    return lax.ppermute(x, axis, pairs)


def turn(x, axis, distance):
    chips = lax.axis_size(axis) // 2
    pairs = [(2 * p + c, 2 * ((p + distance) % chips) + c) for p in range(chips) for c in range(2)]
    return lax.ppermute(x, axis, pairs)


def gather_slabs(x, axis):
    chips = lax.axis_size(axis) // 2
    if chips == 4:
        one, three = turn(x, axis, 1), turn(x, axis, 3)
        return [x, one, turn(one, axis, 1), three]
    return [x] + [turn(x, axis, t) for t in range(1, chips)]


def gather_rows(low, high, axis):
    n = lax.axis_size(axis)
    if n == 4:
        x_high = swap(high, axis, 1)
        y_low = swap(low, axis, 2)
        x_low = swap(low, axis, 1)
        y_high = swap(high, axis, 2)
        d_low = swap(y_low, axis, 1)
        d_high = swap(x_high, axis, 2)
        return [low, high, x_low, x_high, y_low, y_high, d_low, d_high]
    pieces = [jnp.concatenate([low, high], 0)]
    bit = 1
    while bit < n:
        pieces = pieces + [swap(piece, axis, bit) for piece in pieces]
        bit *= 2
    return pieces


def scatter_rows(chunks, axis):
    n = lax.axis_size(axis)
    if n == 4:
        (own_low, own_high), (x_low, x_high), (y_low, y_high), (d_low, d_high) = chunks
        for_y = swap(d_low, axis, 1)
        for_x = swap(d_high, axis, 2)
        from_x = swap(x_low, axis, 1)
        from_y = swap(y_high, axis, 2)
        x_high, y_low = call(pair_kernel, [shape(x_high.shape, BF16)] * 2, [x_high, for_x, y_low, for_y])
        more_x = swap(x_high, axis, 1)
        more_y = swap(y_low, axis, 2)
        return [own_low, from_x, more_y], [own_high, more_x, from_y]
    lows, highs = [], []
    for r, (low, high) in enumerate(chunks):
        lows.append(swap(low, axis, r) if r else low)
        highs.append(swap(high, axis, r) if r else high)
    return lows, highs


def norm_kernel(tok_hbm, cot_hbm, scale_hbm, shift_hbm, gate_hbm, *refs):
    outs, (tok_ref, cot_ref, scale_ref, shift_ref, gate_ref, sems) = refs[:4], refs[4:]
    pairs = (
        (tok_hbm, tok_ref),
        (scale_hbm, scale_ref),
        (shift_hbm, shift_ref),
        (cot_hbm, cot_ref),
        (gate_hbm, gate_ref),
    )
    copies = [pltpu.make_async_copy(src, dst, sems.at[k]) for k, (src, dst) in enumerate(pairs)]
    for copy in copies:
        copy.start()
    for copy in copies[:3]:
        copy.wait()
    half = tok_ref.shape[0] // 2
    for k in range(2):
        at = slice(k * half, (k + 1) * half)
        x = tok_ref[at].astype(F32)
        c = x - jnp.mean(x, 1, keepdims=True)
        var = jnp.mean(c * c, 1, keepdims=True)
        normal = c * lax.rsqrt(var + EPS)
        outs[k][...] = (normal * (1.0 + scale_ref[...]) + shift_ref[...]).astype(BF16)
    for copy in copies[3:]:
        copy.wait()
    for k in range(2):
        at = slice(k * half, (k + 1) * half)
        outs[2 + k][...] = (cot_ref[at].astype(F32) * gate_ref[...]).astype(BF16)


def relative_row(index, e, shift):
    return index ^ (e << shift)


def project_kernel(cfg, sc_ref, idx_ref, *refs):
    chips, pieces, heads, rows = cfg["chips"], cfg["pieces"], cfg["heads"], cfg["rows"]
    ws = refs[: 2 * chips]
    ns = refs[2 * chips : 2 * chips + pieces]
    q_ref, kv_ref, edge_ref, wq_ref = refs[2 * chips + pieces :]
    e, slab = sc_ref[0], sc_ref[1]
    p, c = slab // 2, slab % 2
    wr = ws[0].shape[0]
    for side in range(2):
        for t in range(chips):
            j = 2 * lax.rem(p - t + chips, chips) + (c ^ side)
            block = ws[side * chips + t]
            at = pl.multiple_of(j * wr, wr)
            wq_ref[pl.ds(at, wr), :] = block[...]
    proj = mm(joined(ns), wq_ref[...]).astype(BF16)
    for h in range(heads):
        q = proj[:, 3 * HD * h : 3 * HD * h + HD] * jnp.asarray(HD ** (-0.5), BF16)
        q_ref[h] = jnp.concatenate([q, jnp.zeros_like(q)], 1)
        kv_ref[h] = proj[:, 3 * HD * h + HD : 3 * HD * (h + 1)]
    want = relative_row(idx_ref[...], e, cfg["shift"])
    one_hot = (lax.broadcasted_iota(jnp.int32, (want.shape[0], rows), 1) == want).astype(F32).astype(BF16)
    for h in range(heads):
        edge_ref[h] = mm(one_hot, kv_ref[h]).astype(BF16)


def lives(cfg, sc_ref, v):
    per, shift, win = cfg["per"], cfg["shift"], cfg["win"]
    e = sc_ref[0]
    count = sc_ref[2 + ((e // per) ^ v)]
    low = (e % per) << shift
    live_q = (lax.broadcasted_iota(jnp.int32, (1, win), 1) ^ low) < count
    live_k = (lax.broadcasted_iota(jnp.int32, (win, 1), 0) ^ low) < count
    return live_q, live_k


def units(heads, windows, body):
    group = 2 if heads % 2 == 0 else 1

    def step(k, carry):
        live = [body(k * group + i, v) for i in range(group) for v in range(windows)]
        while live:
            live = [stages for stages in live if next(stages, None)]
        return carry

    lax.fori_loop(0, heads // group, step, 0)


def sized(h, count):
    return pl.ds(pl.multiple_of(h * count, count), count)


def own_forward_kernel(cfg, sc_ref, q_ref, kv_ref, p_ref, m_ref, l_ref, o_ref):
    win = cfg["win"]
    live = [lives(cfg, sc_ref, v)[1] for v in range(cfg["windows"])]

    def body(h, v):
        at = slice(v * win, (v + 1) * win)
        kv = kv_ref[h, at, :]
        s = jnp.where(live[v], mm(kv, q_ref[h, at, :], NT), -1000000000.0)
        yield True
        m = jnp.max(s, 0, keepdims=True)
        yield True
        p = jnp.exp(s - m)
        pb = p.astype(BF16)
        yield True
        m_ref[h, v] = m
        l_ref[h, v] = jnp.sum(p, 0, keepdims=True)
        p_ref[h, v] = pb
        o_ref[h, v] = mm(kv.T, pb)[HD:]

    units(q_ref.shape[0], cfg["windows"], body)


def scaled(g, by):
    part = (g * by).astype(BF16)
    return jnp.concatenate([jnp.zeros_like(part), part], 0)


def edge_kernel(cfg, sc_ref, q_ref, edge_ref, m_ref, l_ref, o_ref, *refs):
    windows, win, edges = cfg["windows"], cfg["win"], cfg["edges"]
    chips, wcol = cfg["chips"], cfg["wcol"]
    wo, ups = refs[:chips], refs[chips:-7]
    att_ref, dedge_ref, dq_ref, g_ref, delta_ref, ga_ref, wos_ref = refs[-7:]
    chip, core = sc_ref[1] // 2, sc_ref[1] % 2
    up = joined(ups)
    aligned = wcol % 128 == 0
    for t in range(chips):
        for side in range(2):
            j = 2 * lax.rem(chip - t + chips, chips) + (core ^ side)
            if aligned:
                wos_ref[:, sized(j, wcol)] = wo[t][side]
            else:
                wos_ref[j] = wo[t][side]
    if aligned:
        ga_ref[...] = mm(wos_ref[...], up, NT)
    else:
        total = None
        for j in range(2 * chips):
            term = mm(wos_ref[j], up[:, j * wcol : (j + 1) * wcol], NT)
            total = term if total is None else total + term
        ga_ref[...] = total

    live = [lives(cfg, sc_ref, v)[0].astype(F32) for v in range(windows)]
    place = [(sc_ref[0] // cfg["per"]) ^ v for v in range(windows)]
    has_edges = sc_ref[1] > 0

    def body(h, v):
        at = slice(v * win, (v + 1) * win)
        kv = edge_ref[h, sized(place[v], edges), :]
        q = q_ref[h, at, :]
        s = jnp.where(has_edges, mm(kv, q, NT), -1000000000.0)
        yield True
        m_edge = jnp.max(s, 0, keepdims=True)
        p = jnp.exp(s - m_edge)
        m_own = m_ref[h, v]
        m = jnp.maximum(m_own, m_edge)
        a, b = jnp.exp(m_own - m), jnp.exp(m_edge - m)
        inv = 1.0 / (a * l_ref[h, v] + b * jnp.sum(p, 0, keepdims=True))
        a, b = a * inv, b * inv
        kv_t = kv.T
        pb = p.astype(BF16)
        yield True
        o = a * o_ref[h, v] + b * mm(kv_t, pb)[HD:]
        att_ref[sized(h, HD), at] = (o * live[v]).astype(BF16)
        gb = (ga_ref[sized(h, HD), at] * live[v]).astype(BF16)
        g = gb.astype(F32)
        delta = jnp.sum(g * o, 0, keepdims=True)
        g_pad = scaled(g, b)
        yield True
        ds = (p * (mm(kv, g_pad) - b * delta)).astype(BF16)
        yield True
        dedge_ref[h, sized(place[v], edges), :] = (mm(ds, q) + mm(pb, g_pad.T)).astype(BF16)
        dq_ref[h, v] = mm(kv_t, ds)[:HD]
        g_ref[h, v] = (g * a).astype(BF16)
        delta_ref[h, v] = a * delta

    units(q_ref.shape[0], windows, body)


def own_backward_kernel(cfg, sc_ref, q_ref, kv_ref, p_ref, g_ref, delta_ref, dqe_ref, dq_ref, dkv_ref):
    win = cfg["win"]

    def body(h, v):
        at = slice(v * win, (v + 1) * win)
        kv, pb, g = kv_ref[h, at, :], p_ref[h, v], g_ref[h, v]
        g_pad = jnp.concatenate([jnp.zeros_like(g), g], 0)
        dp = mm(kv, g_pad)
        yield True
        ds = (pb.astype(F32) * (dp - delta_ref[h, v])).astype(BF16)
        yield True
        dkv_ref[h, at, :] = mm(ds, q_ref[h, at, :]) + mm(pb, g_pad.T)
        dq_t = (mm(kv.T, ds)[:HD] + dqe_ref[h, v]) * (HD ** (-0.5))
        dq_ref[h, at, :] = dq_t.T.astype(BF16)

    units(q_ref.shape[0], cfg["windows"], body)


def place(sc_ref, j, chips):
    chip, core = sc_ref[1] // 2, sc_ref[1] % 2
    return ((j % 2) ^ core) ^ 1, lax.rem(j // 2 - chip + chips, chips)


def weights_in_kernel(cfg, sc_ref, idx_ref, edge_ref, dq_ref, dkv_ref, out_parts_ref, *refs):
    heads, rows = cfg["heads"], cfg["rows"]
    ns, (gp_ref, out_ref) = refs[:-2], refs[-2:]
    want = relative_row(idx_ref[...], sc_ref[0], cfg["shift"])
    one_hot = (lax.broadcasted_iota(jnp.int32, (rows, want.shape[1]), 0) == want).astype(F32).astype(BF16)
    for h in range(heads):
        pair = (dkv_ref[h] + mm(one_hot, edge_ref[h])).astype(BF16)
        gp_ref[:, 3 * HD * h : 3 * HD * (h + 1)] = jnp.concatenate([dq_ref[h], pair], 1)
    chips, wr = out_ref.shape[1], out_ref.shape[2]
    total = mm(joined(ns), gp_ref[...], TN).astype(BF16)
    qw = gp_ref.shape[1]
    for j in range(2 * chips):
        side, t = place(sc_ref, j, chips)
        out_ref[side, t, :, :qw] = total[j * wr : (j + 1) * wr]
    for side in range(2):
        for t in range(chips):
            for k in range(out_parts_ref.shape[2] // wr):
                out_ref[side, t, :, qw + k * wr : qw + (k + 1) * wr] = out_parts_ref[side, t, k * wr : (k + 1) * wr]


def partials_kernel(gp_ref, wq_ref, *outs):
    half = outs[0].shape[0]
    total = mm(gp_ref[...], wq_ref[...], NT).astype(BF16)
    for k, out in enumerate(outs):
        out[...] = total[k * half : (k + 1) * half]


def join_kernel(a_ref, b_ref, out_ref):
    out_ref[...] = (a_ref[...].astype(F32) + b_ref[...].astype(F32)).astype(BF16)


def pair_kernel(a_ref, b_ref, c_ref, d_ref, ab_ref, cd_ref):
    ab_ref[...] = (a_ref[...].astype(F32) + b_ref[...].astype(F32)).astype(BF16)
    cd_ref[...] = (c_ref[...].astype(F32) + d_ref[...].astype(F32)).astype(BF16)


def weights_out_kernel(sc_ref, att_ref, *refs):
    us, out_ref = refs[:-1], refs[-1]
    chips, wr = out_ref.shape[1], out_ref.shape[3]
    total = mm(att_ref[...], joined(us)).astype(BF16)
    for j in range(2 * chips):
        side, t = place(sc_ref, j, chips)
        out_ref[side, t] = total[:, j * wr : (j + 1) * wr]


def add_kernel(mine_ref, other_ref, *outs):
    for t, out in enumerate(outs):
        out[...] = (mine_ref[1, t].astype(F32) + other_ref[t].astype(F32)).astype(BF16)


def final_kernel(tok_ref, cot_ref, scale_ref, *refs):
    parts, out_ref = refs[:-1], refs[-1]
    half, each = tok_ref.shape[0] // 2, len(parts) // 2
    for k in range(2):
        at = slice(k * half, (k + 1) * half)
        x = tok_ref[at].astype(F32)
        c = x - jnp.mean(x, 1, keepdims=True)
        inv = lax.rsqrt(jnp.mean(c * c, 1, keepdims=True) + EPS)
        normal = c * inv
        total = parts[k * each][...].astype(F32)
        for part in parts[k * each + 1 : (k + 1) * each]:
            total = total + part[...].astype(F32)
        hat = total * (1.0 + scale_ref[...])
        grad = hat - jnp.mean(hat, 1, keepdims=True) - normal * jnp.mean(hat * normal, 1, keepdims=True)
        out_ref[at] = (cot_ref[at].astype(F32) + inv * grad).astype(BF16)


def sum_kernel(*refs):
    parts, (q_ref, o_ref) = refs[:-2], refs[-2:]
    total = parts[0][...].astype(F32)
    for part in parts[1:]:
        total = total + part[...].astype(F32)
    wr, qw = q_ref.shape
    q_ref[...] = total[:, :qw]
    for k in range(o_ref.shape[0] // wr):
        o_ref[k * wr : (k + 1) * wr] = total[:, qw + k * wr : qw + (k + 1) * wr]


def shape(dims, dtype):
    return jax.ShapeDtypeStruct(tuple(dims), dtype)


SMEM = pl.BlockSpec(memory_space=pltpu.SMEM)
VMEM = pl.BlockSpec(memory_space=pltpu.VMEM)
HBM = pl.BlockSpec(memory_space=pltpu.HBM)


def call(kernel, outs, operands, scratch=(), limit=32, space=VMEM):
    specs = [SMEM if operand.ndim == 1 else space for operand in operands]
    return pl.pallas_call(
        kernel,
        out_shape=list(outs),
        in_specs=specs,
        out_specs=[VMEM] * len(outs),
        scratch_shapes=list(scratch),
        compiler_params=pltpu.CompilerParams(vmem_limit_bytes=limit * 2**20),
    )(*operands)


def scatter_slabs(parts, chips):
    other = swap(parts[0], "slab", 1)
    dims = parts.shape[2:]
    both = call(add_kernel, [shape(dims, BF16)] * chips, [parts, other])
    if chips == 4:
        passing, last = turn(both[2], "slab", 1), turn(both[3], "slab", 3)
        (joint,) = call(join_kernel, [shape(dims, BF16)], [both[1], passing])
        return [both[0], turn(joint, "slab", 1), last]
    return [both[0]] + [turn(both[t], "slab", t) for t in range(1, chips)]


def program(tokens, cotangent, w_qkv, w_out, mod_scale, mod_shift, mod_gate, counts, edge_index):
    n_enc, n_slab = lax.axis_size("enc"), lax.axis_size("slab")
    chips = n_slab // 2
    own, width = tokens.shape
    rows = own * n_enc
    windows, edges = edge_index.shape
    win = rows // windows
    per = n_enc // windows
    shift = own.bit_length() - 1
    heads = w_out.shape[0] // HD
    qw = w_qkv.shape[1]
    wr = w_qkv.shape[0]

    scale, mod_shift, gate = (a.reshape(1, width) for a in (mod_scale, mod_shift, mod_gate))
    e, slab = lax.axis_index("enc"), lax.axis_index("slab")
    scalars = jnp.concatenate([jnp.stack([e, slab]).astype(jnp.int32), counts])

    ring = gather_slabs(w_qkv, "slab")
    n_low, n_high, u_low, u_high = call(
        norm_kernel,
        [shape((own // 2, width), BF16)] * 4,
        [tokens, cotangent, scale, mod_shift, gate],
        [pltpu.VMEM(tokens.shape, BF16)] * 2 + [pltpu.VMEM((1, width), F32)] * 3 + [pltpu.SemaphoreType.DMA((5,))],
        limit=63,
        space=HBM,
    )
    normed = gather_rows(n_low, n_high, "enc")
    idx_next = hop(edge_index, "slab", -1)
    weights = ring + [swap(block, "slab", 1) for block in ring]
    upstream = gather_rows(u_low, u_high, "enc")
    out_pair = jnp.stack([w_out, swap(w_out, "slab", 1)])
    out_ring = gather_slabs(out_pair, "slab")

    cfg = dict(chips=chips, pieces=len(normed), heads=heads, rows=rows, shift=shift)
    edge_shape = shape((heads, windows * edges, 2 * HD), BF16)
    q, kv, edge_out, wq = call(
        functools.partial(project_kernel, cfg),
        [shape((heads, rows, 2 * HD), BF16)] * 2 + [edge_shape, shape((width, qw), BF16)],
        [scalars, idx_next.reshape(-1, 1), *weights, *normed],
    )
    edge_in = hop(edge_out, "slab", 1)

    cfg = dict(windows=windows, win=win, shift=shift, per=per, edges=edges, chips=chips, wcol=wr)
    line = shape((heads, windows, 1, win), F32)
    across = (heads, windows, HD, win)
    p, m, l, o = call(
        functools.partial(own_forward_kernel, cfg),
        [shape((heads, windows, win, win), BF16), line, line, shape(across, F32)],
        [scalars, q, kv],
    )
    att, dedge, dqe, g, delta = call(
        functools.partial(edge_kernel, cfg),
        [shape((heads * HD, rows), BF16), edge_shape, shape(across, F32), shape(across, BF16), line],
        [scalars, q, edge_in, m, l, o, *out_ring, *upstream],
        [
            pltpu.VMEM((heads * HD, rows), F32),
            pltpu.VMEM((heads * HD, width) if wr % 128 == 0 else (n_slab,) + w_out.shape, BF16),
        ],
    )
    dedge_in = hop(dedge, "slab", -1)
    (out_parts,) = call(weights_out_kernel, [shape((2, chips) + w_out.shape, BF16)], [scalars, att, *upstream])
    dq, dkv = call(
        functools.partial(own_backward_kernel, cfg),
        [shape((heads, rows, HD), BF16), shape((heads, rows, 2 * HD), F32)],
        [scalars, q, kv, p, g, delta, dqe],
    )

    cfg = dict(heads=heads, rows=rows, shift=shift)
    gp, parts = call(
        functools.partial(weights_in_kernel, cfg),
        [shape((rows, qw), BF16), shape((2, chips, wr, qw + w_out.shape[0] // wr * wr), BF16)],
        [scalars, idx_next.reshape(1, -1), dedge_in, dq, dkv, out_parts, *normed],
    )
    arrived = scatter_slabs(parts, chips)
    partial = call(partials_kernel, [shape((own // 2, width), BF16)] * (2 * n_enc), [gp, wq])
    lows, highs = scatter_rows(list(zip(partial[::2], partial[1::2])), "enc")
    grad_qkv, grad_out = call(sum_kernel, [shape(w_qkv.shape, F32), shape(w_out.shape, F32)], arrived)
    (grad_tokens,) = call(final_kernel, [shape(tokens.shape, BF16)], [tokens, cotangent, scale, *lows, *highs])
    return (grad_tokens, grad_qkv, grad_out)


def solution(mesh):
    placed = (
        P(("slab", "enc"), None),
        P(("slab", "enc"), None),
        P("slab", "enc"),
        P("enc", "slab"),
        P(),
        P(),
        P(),
        P("slab"),
        P("slab", None),
    )
    return jax.shard_map(
        program,
        mesh=mesh,
        in_specs=placed,
        out_specs=(P(("slab", "enc"), None), P("slab", "enc"), P("enc", "slab")),
        check_vma=False,
    )
```

```python
import functools
import jax
import jax.numpy as jnp
from jax import lax
from jax.experimental import pallas as pl
from jax.experimental.pallas import tpu as pltpu
from jax.sharding import PartitionSpec as P


HD = 64
EPS = 1e-06
F32 = jnp.float32
BF16 = jnp.bfloat16
NT = (((1,), (1,)), ((), ()))
TN = (((0,), (0,)), ((), ()))


def mm(a, b, dims=(((1,), (0,)), ((), ()))):
    return lax.dot_general(a, b, dims, preferred_element_type=F32)


def joined(refs):
    return jnp.concatenate([ref[...] for ref in refs], 0)


def swap(x, axis, mask):
    return lax.ppermute(x, axis, [(i, i ^ mask) for i in range(lax.axis_size(axis))])


def hop(x, axis, distance):
    n = lax.axis_size(axis)
    pairs = [(i, i + distance) for i in range(n) if 0 <= i + distance < n]
    return lax.ppermute(x, axis, pairs)


def turn(x, axis, distance):
    chips = lax.axis_size(axis) // 2
    pairs = [(2 * p + c, 2 * ((p + distance) % chips) + c) for p in range(chips) for c in range(2)]
    return lax.ppermute(x, axis, pairs)


def gather_slabs(x, axis):
    chips = lax.axis_size(axis) // 2
    if chips == 4:
        one, three = turn(x, axis, 1), turn(x, axis, 3)
        return [x, one, turn(one, axis, 1), three]
    return [x] + [turn(x, axis, t) for t in range(1, chips)]


def gather_rows(low, high, own, axis):
    n = lax.axis_size(axis)
    if n != 4:
        return [own] + [swap(own, axis, r) for r in range(1, n)]
    x_high = swap(high, axis, 1)
    y_low = swap(low, axis, 2)
    x_low = swap(low, axis, 1)
    y_high = swap(high, axis, 2)
    d_low = swap(y_low, axis, 1)
    d_high = swap(x_high, axis, 2)
    return [own, x_low, x_high, y_low, y_high, d_low, d_high]


def scatter_rows(chunks, axis):
    n = lax.axis_size(axis)
    if n == 4:
        (own_low, own_high), (x_low, x_high), (y_low, y_high), (d_low, d_high) = chunks
        for_y = swap(d_low, axis, 1)
        for_x = swap(d_high, axis, 2)
        from_x = swap(x_low, axis, 1)
        from_y = swap(y_high, axis, 2)
        x_high, y_low = call(pair_kernel, [shape(x_high.shape, BF16)] * 2, [x_high, for_x, y_low, for_y])
        more_x = swap(x_high, axis, 1)
        more_y = swap(y_low, axis, 2)
        return [own_low, from_x, more_y], [own_high, more_x, from_y]
    lows, highs = [], []
    for r, (low, high) in enumerate(chunks):
        lows.append(swap(low, axis, r) if r else low)
        highs.append(swap(high, axis, r) if r else high)
    return lows, highs


def norm_kernel(tok_hbm, cot_hbm, scale_hbm, shift_hbm, gate_hbm, *refs):
    normed_refs, up_refs, (own_ref, up_own_ref) = refs[:2], refs[2:4], refs[4:6]
    tok_ref, cot_ref, scale_ref, shift_ref, gate_ref, sems = refs[6:]
    pairs = (
        (tok_hbm, tok_ref),
        (scale_hbm, scale_ref),
        (shift_hbm, shift_ref),
        (cot_hbm, cot_ref),
        (gate_hbm, gate_ref),
    )
    copies = [pltpu.make_async_copy(src, dst, sems.at[k]) for k, (src, dst) in enumerate(pairs)]
    for copy in copies:
        copy.start()
    for copy in copies[:3]:
        copy.wait()
    half = tok_ref.shape[0] // 2
    for k, out in enumerate(normed_refs):
        at = slice(k * half, (k + 1) * half)
        x = tok_ref[at].astype(F32)
        c = x - jnp.mean(x, 1, keepdims=True)
        var = jnp.mean(c * c, 1, keepdims=True)
        normal = c * lax.rsqrt(var + EPS)
        normed = (normal * (1.0 + scale_ref[...]) + shift_ref[...]).astype(BF16)
        out[...] = normed
        own_ref[at] = normed
    for copy in copies[3:]:
        copy.wait()
    for k, out in enumerate(up_refs):
        at = slice(k * half, (k + 1) * half)
        up = (cot_ref[at].astype(F32) * gate_ref[...]).astype(BF16)
        out[...] = up
        up_own_ref[at] = up


def keep_kernel(in_ref, out_ref):
    out_ref[...] = in_ref[...]


def pack_kernel(wq_ref, wo_ref, out_ref):
    wr, qw = wq_ref.shape
    out_ref[:, :qw] = wq_ref[...]
    for k in range(wo_ref.shape[0] // wr):
        out_ref[:, qw + k * wr : qw + (k + 1) * wr] = wo_ref[k * wr : (k + 1) * wr]


def relative_rows(idx_ref, shift):
    index = jnp.concatenate([idx_ref[w : w + 1, :] for w in range(idx_ref.shape[0])], 1)
    return index ^ (lax.axis_index("enc") << shift)


def project_kernel(cfg, idx_ref, *refs):
    chips, heads, rows = cfg["chips"], cfg["heads"], cfg["rows"]
    ws, ns, (q_ref, kv_ref, edge_ref, wq_ref, wo_ref) = refs[: 2 * chips], refs[2 * chips : -5], refs[-5:]
    slab = lax.axis_index("slab")
    p, c = slab // 2, slab % 2
    wr, qw = ws[0].shape[0], wq_ref.shape[1]

    def restore(block, side, t):
        j = 2 * lax.rem(p - t + chips, chips) + (c ^ side)
        wq_ref[sized(j, wr), :] = block[:, :qw]
        if wr % 128 == 0:
            for k in range((block.shape[1] - qw) // wr):
                wo_ref[k * wr : (k + 1) * wr, sized(j, wr)] = block[:, qw + k * wr : qw + (k + 1) * wr]
        else:
            wo_ref[j] = block[:, qw:]

    for k, block in enumerate(ws):
        restore(block, *divmod(k, chips))
    proj = mm(joined(ns), wq_ref[...]).astype(BF16)
    for h in range(heads):
        q = proj[:, 3 * HD * h : 3 * HD * h + HD] * jnp.asarray(HD ** (-0.5), BF16)
        q_ref[h] = jnp.concatenate([q, jnp.zeros_like(q)], 1)
        kv_ref[h] = proj[:, 3 * HD * h + HD : 3 * HD * (h + 1)]
    want = relative_rows(idx_ref, cfg["shift"]).astype(F32)
    want = jnp.broadcast_to(want, (128, want.shape[1])).T[:, :1].astype(jnp.int32)
    one_hot = (lax.broadcasted_iota(jnp.int32, (want.shape[0], rows), 1) == want).astype(F32).astype(BF16)
    for h in range(heads):
        edge_ref[h] = mm(one_hot, kv_ref[h]).astype(BF16)


def lives(cfg, counts_ref, v):
    per, shift, win = cfg["per"], cfg["shift"], cfg["win"]
    e = lax.axis_index("enc")
    count = counts_ref[(e // per) ^ v]
    low = (e % per) << shift
    live_q = (lax.broadcasted_iota(jnp.int32, (1, win), 1) ^ low) < count
    live_k = (lax.broadcasted_iota(jnp.int32, (win, 1), 0) ^ low) < count
    return live_q, live_k


def units(heads, windows, body):
    group = 2 if heads % 2 == 0 else 1

    def step(k, carry):
        live = [body(k * group + i, v) for i in range(group) for v in range(windows)]
        while live:
            live = [stages for stages in live if next(stages, None)]
        return carry

    lax.fori_loop(0, heads // group, step, 0)


def sized(h, count):
    return pl.ds(pl.multiple_of(h * count, count), count)


def own_forward_kernel(cfg, counts_ref, q_ref, kv_ref, p_ref, m_ref, l_ref, o_ref):
    win = cfg["win"]
    live = [lives(cfg, counts_ref, v)[1] for v in range(cfg["windows"])]

    def body(h, v):
        at = slice(v * win, (v + 1) * win)
        kv = kv_ref[h, at, :]
        s = jnp.where(live[v], mm(kv, q_ref[h, at, :], NT), -1000000000.0)
        yield True
        m = jnp.max(s, 0, keepdims=True)
        yield True
        p = jnp.exp(s - m)
        pb = p.astype(BF16)
        yield True
        m_ref[h, v] = m
        l_ref[h, v] = jnp.sum(p, 0, keepdims=True)
        p_ref[h, v] = pb
        o_ref[h, v] = mm(kv.T[HD:], pb)

    units(q_ref.shape[0], cfg["windows"], body)


def scaled(g, by):
    part = (g * by).astype(BF16)
    return jnp.concatenate([jnp.zeros_like(part), part], 0)


def edge_kernel(cfg, counts_ref, q_ref, edge_ref, m_ref, l_ref, o_ref, wo_ref, *refs):
    windows, win, edges = cfg["windows"], cfg["win"], cfg["edges"]
    ups, (att_ref, dedge_ref, dq_ref, g_ref, delta_ref, ga_ref) = refs[:-6], refs[-6:]
    up = joined(ups)
    if wo_ref.ndim == 2:
        ga_ref[...] = mm(wo_ref[...], up, NT)
    else:
        for k in range(wo_ref.shape[2] // wo_ref.shape[1]):
            total, wr = None, wo_ref.shape[1]
            for j in range(wo_ref.shape[0]):
                term = mm(wo_ref[j, :, k * wr : (k + 1) * wr], up[:, j * wr : (j + 1) * wr], NT)
                total = term if total is None else total + term
            ga_ref[k * wr : (k + 1) * wr] = total

    live = [lives(cfg, counts_ref, v)[0].astype(F32) for v in range(windows)]
    place = [(lax.axis_index("enc") // cfg["per"]) ^ v for v in range(windows)]
    has_edges = lax.axis_index("slab") > 0

    def body(h, v):
        at = slice(v * win, (v + 1) * win)
        kv = edge_ref[h, sized(place[v], edges), :]
        q = q_ref[h, at, :]
        s = jnp.where(has_edges, mm(kv, q, NT), -1000000000.0)
        yield True
        m_edge = jnp.max(s, 0, keepdims=True)
        p = jnp.exp(s - m_edge)
        m_own = m_ref[h, v]
        m = jnp.maximum(m_own, m_edge)
        a, b = jnp.exp(m_own - m), jnp.exp(m_edge - m)
        inv = 1.0 / (a * l_ref[h, v] + b * jnp.sum(p, 0, keepdims=True))
        a, b = a * inv, b * inv
        kv_t = kv.T
        pb = p.astype(BF16)
        yield True
        o = a * o_ref[h, v] + b * mm(kv_t, pb)[HD:]
        att_ref[sized(h, HD), at] = (o * live[v]).astype(BF16)
        gb = (ga_ref[sized(h, HD), at] * live[v]).astype(BF16)
        g = gb.astype(F32)
        delta = jnp.sum(g * o, 0, keepdims=True)
        g_pad = scaled(g, b)
        yield True
        ds = (p * (mm(kv, g_pad) - b * delta)).astype(BF16)
        yield True
        dedge_ref[h, sized(place[v], edges), :] = (mm(ds, q) + mm(pb, g_pad.T)).astype(BF16)
        dq_ref[h, v] = mm(kv_t, ds)[:HD]
        g_ref[h, v] = (g * a).astype(BF16)
        delta_ref[h, v] = a * delta

    units(q_ref.shape[0], windows, body)


def own_backward_kernel(cfg, q_ref, kv_ref, p_ref, g_ref, delta_ref, dqe_ref, dq_ref, dkv_ref):
    win = cfg["win"]

    def body(h, v):
        at = slice(v * win, (v + 1) * win)
        kv, pb, g = kv_ref[h, at, :], p_ref[h, v], g_ref[h, v]
        g_pad = jnp.concatenate([jnp.zeros_like(g), g], 0)
        dp = mm(kv, g_pad)
        yield True
        ds = (pb.astype(F32) * (dp - delta_ref[h, v])).astype(BF16)
        yield True
        dkv_ref[h, at, :] = mm(ds, q_ref[h, at, :]) + mm(pb, g_pad.T)
        dq_t = (mm(kv.T, ds)[:HD] + dqe_ref[h, v]) * (HD ** (-0.5))
        dq_ref[h, at, :] = dq_t.T.astype(BF16)

    units(q_ref.shape[0], cfg["windows"], body)


def place(j, chips):
    slab = lax.axis_index("slab")
    chip, core = slab // 2, slab % 2
    return ((j % 2) ^ core) ^ 1, lax.rem(j // 2 - chip + chips, chips)


def weights_in_kernel(cfg, idx_ref, edge_ref, dq_ref, dkv_ref, out_parts_ref, *refs):
    heads, rows = cfg["heads"], cfg["rows"]
    ns, (gp_ref, out_ref) = refs[:-2], refs[-2:]
    want = relative_rows(idx_ref, cfg["shift"])
    one_hot = (lax.broadcasted_iota(jnp.int32, (rows, want.shape[1]), 0) == want).astype(F32).astype(BF16)
    for h in range(heads):
        pair = (dkv_ref[h] + mm(one_hot, edge_ref[h])).astype(BF16)
        gp_ref[:, 3 * HD * h : 3 * HD * (h + 1)] = jnp.concatenate([dq_ref[h], pair], 1)
    chips, wr = out_ref.shape[1], out_ref.shape[2]
    total = mm(joined(ns), gp_ref[...], TN).astype(BF16)
    qw = gp_ref.shape[1]
    for j in range(2 * chips):
        side, t = place(j, chips)
        out_ref[side, t, :, :qw] = total[j * wr : (j + 1) * wr]
    for side in range(2):
        for t in range(chips):
            for k in range(out_parts_ref.shape[2] // wr):
                out_ref[side, t, :, qw + k * wr : qw + (k + 1) * wr] = out_parts_ref[side, t, k * wr : (k + 1) * wr]


def partials_kernel(gp_ref, wq_ref, *outs):
    half = outs[0].shape[0]
    total = mm(gp_ref[...], wq_ref[...], NT).astype(BF16)
    for k, out in enumerate(outs):
        out[...] = total[k * half : (k + 1) * half]


def join_kernel(a_ref, b_ref, out_ref):
    out_ref[...] = (a_ref[...].astype(F32) + b_ref[...].astype(F32)).astype(BF16)


def pair_kernel(a_ref, b_ref, c_ref, d_ref, ab_ref, cd_ref):
    ab_ref[...] = (a_ref[...].astype(F32) + b_ref[...].astype(F32)).astype(BF16)
    cd_ref[...] = (c_ref[...].astype(F32) + d_ref[...].astype(F32)).astype(BF16)


def weights_out_kernel(att_ref, *refs):
    us, out_ref = refs[:-1], refs[-1]
    chips, wr = out_ref.shape[1], out_ref.shape[3]
    total = mm(att_ref[...], joined(us)).astype(BF16)
    for j in range(2 * chips):
        side, t = place(j, chips)
        out_ref[side, t] = total[:, j * wr : (j + 1) * wr]


def add_kernel(mine_ref, other_ref, *outs):
    for t, out in enumerate(outs):
        out[...] = (mine_ref[1, t].astype(F32) + other_ref[t].astype(F32)).astype(BF16)


def final_kernel(tok_ref, cot_ref, scale_ref, *refs):
    parts, out_ref = refs[:-1], refs[-1]
    half, each = tok_ref.shape[0] // 2, len(parts) // 2
    for k in range(2):
        at = slice(k * half, (k + 1) * half)
        x = tok_ref[at].astype(F32)
        c = x - jnp.mean(x, 1, keepdims=True)
        inv = lax.rsqrt(jnp.mean(c * c, 1, keepdims=True) + EPS)
        normal = c * inv
        total = parts[k * each][...].astype(F32)
        for part in parts[k * each + 1 : (k + 1) * each]:
            total = total + part[...].astype(F32)
        hat = total * (1.0 + scale_ref[...])
        grad = hat - jnp.mean(hat, 1, keepdims=True) - normal * jnp.mean(hat * normal, 1, keepdims=True)
        out_ref[at] = (cot_ref[at].astype(F32) + inv * grad).astype(BF16)


def sum_kernel(*refs):
    parts, (q_ref, o_ref) = refs[:-2], refs[-2:]
    total = parts[0][...].astype(F32)
    for part in parts[1:]:
        total = total + part[...].astype(F32)
    wr, qw = q_ref.shape
    q_ref[...] = total[:, :qw]
    for k in range(o_ref.shape[0] // wr):
        o_ref[k * wr : (k + 1) * wr] = total[:, qw + k * wr : qw + (k + 1) * wr]


def shape(dims, dtype):
    return jax.ShapeDtypeStruct(tuple(dims), dtype)


SMEM = pl.BlockSpec(memory_space=pltpu.SMEM)
VMEM = pl.BlockSpec(memory_space=pltpu.VMEM)
HBM = pl.BlockSpec(memory_space=pltpu.HBM)


def call(kernel, outs, operands, scratch=(), limit=32, raw=()):
    specs = [SMEM if operand.ndim == 1 else HBM if k in raw else VMEM for k, operand in enumerate(operands)]
    return pl.pallas_call(
        kernel,
        out_shape=list(outs),
        in_specs=specs,
        out_specs=[VMEM] * len(outs),
        scratch_shapes=list(scratch),
        compiler_params=pltpu.CompilerParams(vmem_limit_bytes=limit * 2**20),
    )(*operands)


def scatter_slabs(parts, chips):
    other = swap(parts[0], "slab", 1)
    dims = parts.shape[2:]
    both = call(add_kernel, [shape(dims, BF16)] * chips, [parts, other])
    if chips == 4:
        passing, last = turn(both[2], "slab", 1), turn(both[3], "slab", 3)
        (joint,) = call(join_kernel, [shape(dims, BF16)], [both[1], passing])
        return [both[0], turn(joint, "slab", 1), last]
    return [both[0]] + [turn(both[t], "slab", t) for t in range(1, chips)]


def program(tokens, cotangent, w_qkv, w_out, mod_scale, mod_shift, mod_gate, counts, edge_index):
    n_enc, n_slab = lax.axis_size("enc"), lax.axis_size("slab")
    chips = n_slab // 2
    own, width = tokens.shape
    rows = own * n_enc
    windows, edges = edge_index.shape
    win = rows // windows
    per = n_enc // windows
    shift = own.bit_length() - 1
    heads = w_out.shape[0] // HD
    qw = w_qkv.shape[1]
    wr = w_qkv.shape[0]

    scale, mod_shift, gate = (a.reshape(1, width) for a in (mod_scale, mod_shift, mod_gate))
    idx_next = hop(edge_index, "slab", -1)
    packed_shape = shape((wr, qw + w_out.shape[0] // wr * wr), BF16)
    half = shape((own // 2, width), BF16)
    n_low, n_high, u_low, u_high, n_own, u_own = call(
        norm_kernel,
        [half] * 4 + [shape(tokens.shape, BF16)] * 2,
        [tokens, cotangent, scale, mod_shift, gate],
        [pltpu.VMEM(tokens.shape, BF16)] * 2 + [pltpu.VMEM((1, width), F32)] * 3 + [pltpu.SemaphoreType.DMA((5,))],
        limit=63,
        raw=range(5),
    )
    (n_own,) = call(keep_kernel, [shape(n_own.shape, BF16)], [n_own])
    normed = gather_rows(n_low, n_high, n_own, "enc")
    (packed,) = call(pack_kernel, [packed_shape], [w_qkv, w_out])
    ring = gather_slabs(packed, "slab")
    upstream = gather_rows(u_low, u_high, u_own, "enc")
    weights = ring + [swap(block, "slab", 1) for block in ring]

    cfg = dict(chips=chips, heads=heads, rows=rows, shift=shift)
    edge_shape = shape((heads, windows * edges, 2 * HD), BF16)
    wo_dims = (w_out.shape[0], width) if wr % 128 == 0 else (n_slab, wr, packed.shape[1] - qw)
    q, kv, edge_out, wq, wo = call(
        functools.partial(project_kernel, cfg),
        [shape((heads, rows, 2 * HD), BF16)] * 2 + [edge_shape, shape((width, qw), BF16), shape(wo_dims, BF16)],
        [idx_next, *weights, *normed],
    )
    edge_in = hop(edge_out, "slab", 1)

    cfg = dict(windows=windows, win=win, shift=shift, per=per, edges=edges)
    line = shape((heads, windows, 1, win), F32)
    across = (heads, windows, HD, win)
    p, m, l, o = call(
        functools.partial(own_forward_kernel, cfg),
        [shape((heads, windows, win, win), BF16), line, line, shape(across, F32)],
        [counts, q, kv],
    )
    att, dedge, dqe, g, delta = call(
        functools.partial(edge_kernel, cfg),
        [shape((heads * HD, rows), BF16), edge_shape, shape(across, F32), shape(across, BF16), line],
        [counts, q, edge_in, m, l, o, wo, *upstream],
        [pltpu.VMEM((heads * HD, rows), F32)],
    )
    dedge_in = hop(dedge, "slab", -1)
    (out_parts,) = call(weights_out_kernel, [shape((2, chips) + w_out.shape, BF16)], [att, *upstream])
    dq, dkv = call(
        functools.partial(own_backward_kernel, cfg),
        [shape((heads, rows, HD), BF16), shape((heads, rows, 2 * HD), F32)],
        [q, kv, p, g, delta, dqe],
    )

    cfg = dict(heads=heads, rows=rows, shift=shift)
    gp, parts = call(
        functools.partial(weights_in_kernel, cfg),
        [shape((rows, qw), BF16), shape((2, chips) + packed.shape, BF16)],
        [idx_next, dedge_in, dq, dkv, out_parts, *normed],
    )
    arrived = scatter_slabs(parts, chips)
    partial = call(partials_kernel, [shape((own // 2, width), BF16)] * (2 * n_enc), [gp, wq])
    lows, highs = scatter_rows(list(zip(partial[::2], partial[1::2])), "enc")
    grad_qkv, grad_out = call(sum_kernel, [shape(w_qkv.shape, F32), shape(w_out.shape, F32)], arrived)
    (grad_tokens,) = call(final_kernel, [shape(tokens.shape, BF16)], [tokens, cotangent, scale, *lows, *highs])
    return (grad_tokens, grad_qkv, grad_out)


def solution(mesh):
    placed = (
        P(("slab", "enc"), None),
        P(("slab", "enc"), None),
        P("slab", "enc"),
        P("enc", "slab"),
        P(),
        P(),
        P(),
        P("slab"),
        P("slab", None),
    )
    return jax.shard_map(
        program,
        mesh=mesh,
        in_specs=placed,
        out_specs=(P(("slab", "enc"), None), P("slab", "enc"), P("enc", "slab")),
        check_vma=False,
    )
```
